128 devices in a mesh: grp: 4 (over z), ctx: 32 (over x, y, core).
Axes of the slice: x: 4, y: 4, z: 4, core: 2. Of those that a mesh axis runs over, the one named last changes fastest.
Arguments:
- queries: bfloat16 [49152, 1024], P(('grp', 'ctx')), may hold values from -10 to 10
- keys_cache: bfloat16 [16384, 128, 128], P(('grp', 'ctx')), may hold values from -8 to 8
- values_cache: bfloat16 [16384, 128, 128], P(('grp', 'ctx')), may hold values from -6 to 6
- block_list: int32 [384, 36], P(('grp', 'ctx')), may hold values from 0 to 16383, as said below
- page_table: int32 [16384], replicated, may hold values from 0 to 16383, as said below
Outputs:
- attended: bfloat16 [49152, 1024], P(('grp', 'ctx'))
The draws below stay inside these ranges and needn't reach their ends.
Inputs may be any that keep to these rules, and one draw needn't show every extreme that they name: `block_list`: each tile's 36 listed blocks are distinct. Page p is row p of keys_cache and values_cache. Through page_table, each tile lists exactly 9 blocks stored on the devices of each index of grp. Over the 3 tiles of one device and one index of grp, at most 3 listed blocks are stored on any one device, and in every draw, for every device and every group, some device of that group stores exactly 3 of them. `page_table`: each page once.
All inputs are finite; a program needn't handle non-finite values.
Results may differ from the reference program's by a relative error of at most 0.0045.
Values may be sent and summed in bfloat16 or wider, within the bound.
A program may use at most 192 MiB of HBM per device.

```python
import jax
import jax.numpy as jnp
from jax import lax

HD = 128
HEADS = 8
BLOCK = 128
NB = 36
TILE_DEV = 3
BLK_DEV = 128
PER_GRP = 9
CAP = 3
TILES = 384
TOKENS = 49152
PAGES = 16384


def draw_queries(key, part):
    sub_key = jax.random.fold_in(key, 11)
    filled = jnp.clip(2.5 * jax.random.normal(sub_key, (TOKENS, HEADS * HD), jnp.float32), -10.0, 10.0)
    return filled.astype(jnp.bfloat16)


def draw_keys_cache(key, part):
    sub_key = jax.random.fold_in(key, 23)
    filled = jnp.clip(jax.random.normal(sub_key, (PAGES, BLOCK, HD), jnp.float32), -6.0, 6.0)
    return filled.astype(jnp.bfloat16)


def listing(key):
    groups = NB // PER_GRP
    devices = PAGES // BLK_DEV
    owners_count = devices // groups
    requests = TILE_DEV * PER_GRP
    slot_count = owners_count * CAP
    base_key = jax.random.fold_in(key, 505)
    page_table = jax.random.permutation(jax.random.fold_in(base_key, 1), PAGES).astype(jnp.int32)
    busiest = jax.random.randint(jax.random.fold_in(base_key, 2), (groups,), 0, owners_count)
    jitter = jax.random.randint(jax.random.fold_in(base_key, 3), (devices, groups, slot_count), 0, 1 << 20)
    slot_ids = jnp.arange(slot_count, dtype=jnp.int32)
    owner_of = slot_ids // CAP
    is_hot = (owner_of[None, None, :] == busiest[None, :, None]).astype(jnp.int32)
    ranked = (jitter + is_hot * (1 << 20)) * slot_count + slot_ids[None, None, :]
    ranking = jnp.argsort(ranked, axis=-1)
    chosen_owner = owner_of[ranking[:, :, :requests - CAP]]
    hot_owner = jnp.broadcast_to(busiest[None, :, None], (devices, groups, CAP))
    owners = jnp.concatenate([hot_owner, chosen_owner], axis=-1)
    jitter_two = jax.random.randint(jax.random.fold_in(base_key, 4), (devices, groups, requests), 0, 1 << 20)
    shuffle = jnp.argsort(jitter_two * requests + jnp.arange(requests, dtype=jnp.int32)[None, None, :], axis=-1)
    owners = jnp.take_along_axis(owners, shuffle, axis=-1).reshape(devices, groups, TILE_DEV, PER_GRP)
    offset = jax.random.randint(jax.random.fold_in(base_key, 5), (devices, groups, TILE_DEV, 1), 0, BLK_DEV)
    in_device = (offset + 7 * jnp.arange(PER_GRP, dtype=jnp.int32)[None, None, None, :]) % BLK_DEV
    group_index = jnp.arange(groups, dtype=jnp.int32)[None, :, None, None]
    page_ids = (group_index * owners_count + owners) * BLK_DEV + in_device
    page_ids = page_ids.transpose(0, 2, 1, 3).reshape(TILES, NB)
    jitter_three = jax.random.randint(jax.random.fold_in(base_key, 6), (TILES, NB), 0, 1 << 20)
    spread = jnp.argsort(jitter_three * NB + jnp.arange(NB, dtype=jnp.int32)[None, :], axis=-1)
    page_ids = jnp.take_along_axis(page_ids, spread, axis=-1)
    inverse = jnp.zeros((PAGES,), jnp.int32).at[page_table].set(jnp.arange(PAGES, dtype=jnp.int32))
    block_list = inverse[page_ids].astype(jnp.int32)
    return (block_list, page_table)


def draw_block_list(key, part):
    return listing(key)[0]


def draw_page_table(key, part):
    return listing(key)[1]


def block_levels(key, dims, pieces, least, high):
    def one(dim, blocks):
        steps = jax.random.uniform(jax.random.fold_in(jax.random.fold_in(key, 6), dim), (blocks,), jnp.float32, least / len(pieces), high / len(pieces))
        return jnp.repeat(jnp.exp(steps), dims[dim] // blocks).reshape((-1,) + (1,) * (len(dims) - dim - 1))

    loudness = one(*pieces[0])
    for cut in pieces[1:]:
        loudness = loudness * one(*cut)
    return loudness


def scatter_about(rng, extent, scale, limit, pieces=(), held_as=jnp.bfloat16):
    values = scale * jax.random.normal(rng, extent, jnp.float32)
    if pieces:
        values = values * block_levels(rng, extent, pieces, -0.22, 0.18)
    return jnp.clip(values, -limit, limit).astype(held_as)


def setup_inputs(seed: int = 0) -> dict:
    streams_of = jax.random.split(jax.random.key(seed), 6)
    queries = draw_queries(jax.random.fold_in(streams_of[5], 71), 0)
    keys_cache = draw_keys_cache(jax.random.fold_in(streams_of[5], 71), 0)
    values_cache = scatter_about(streams_of[2], (PAGES, BLOCK, HD), 1.0, 6.0, ((0, 128),))
    block_list = draw_block_list(jax.random.fold_in(streams_of[5], 71), 0)
    page_table = draw_page_table(jax.random.fold_in(streams_of[5], 71), 0)
    return {"queries": queries, "keys_cache": keys_cache, "values_cache": values_cache, "block_list": block_list, "page_table": page_table}


def reference(queries, keys_cache, values_cache, block_list, page_table):
    scaling = HD ** -0.5
    query_tiles = queries.reshape(TILES, BLOCK, HEADS, HD)

    def attend_tile(operands):
        tile_rows, listed = operands
        page_ids = page_table[listed].astype(jnp.int32)
        tile_keys = keys_cache[page_ids].reshape(NB * BLOCK, HD)
        tile_values = values_cache[page_ids].reshape(NB * BLOCK, HD)
        stacked = tile_rows.transpose(1, 0, 2).reshape(HEADS * BLOCK, HD)
        scores = jnp.dot(stacked, tile_keys.T, preferred_element_type=jnp.float32) * scaling
        largest = jnp.max(scores, axis=1, keepdims=True)
        weights = jnp.exp(scores - largest)
        denominator = jnp.sum(weights, axis=1)
        summed = jnp.dot(weights.astype(jnp.bfloat16), tile_values, preferred_element_type=jnp.float32)
        result = summed / denominator[:, None]
        result = result.reshape(HEADS, BLOCK, HD).transpose(1, 0, 2).reshape(BLOCK, HEADS * HD)
        return result.astype(jnp.bfloat16)

    attended = lax.map(attend_tile, (query_tiles, block_list))
    return attended.reshape(TOKENS, HEADS * HD)
```

```python
import functools
import math

import jax
import jax.numpy as jnp
from jax import lax
from jax.experimental import pallas as pl
from jax.experimental.pallas import tpu as pltpu
from jax.sharding import PartitionSpec as P

HD = 128
HEADS = 8
BLOCK = 128
NB = 36
TILE_DEV = 3
BLK_DEV = 128
CAP = 3
PLANES = 4
CTX = 32
PER_GRP = NB // PLANES
KEYS = PER_GRP * BLOCK
ROWS = HEADS * BLOCK
PAIR = 2 * BLOCK
PAIRS = ROWS // PAIR
ITEMS = TILE_DEV * PAIRS
WINDOW = 16
AHEAD = 15
PEERS = CTX - 1
PLANE_STEPS = (1, 3, 2, 0)
STATS = BLOCK + 8
MESH = pl.DeviceIdType.MESH
SCALE2 = HD**-0.5 * math.log2(math.e)


def request_plan(page_ids):
    flat = page_ids.reshape(-1)
    device_of, within = flat // BLK_DEV, flat % BLK_DEV
    position = jnp.arange(flat.shape[0], dtype=jnp.int32)
    earlier = position[None, :] < position[:, None]
    rank = jnp.sum(((device_of[None, :] == device_of[:, None]) & earlier).astype(jnp.int32), axis=1)
    devices = jnp.arange(PLANES * CTX, dtype=jnp.int32)
    ranks = jnp.arange(CAP, dtype=jnp.int32)
    place = (device_of * CAP + rank)[None, None, :] == (devices[:, None] * CAP + ranks)[:, :, None]
    wanted = jnp.sum(jnp.where(place, within[None, None, :], 0), axis=2)
    tile = position // NB
    plane = device_of // CTX
    same = (plane[None, :] == plane[:, None]) & (tile[None, :] == tile[:, None]) & earlier
    order = jnp.sum(same.astype(jnp.int32), axis=1)
    slot = (device_of % CTX) * CAP + rank
    key = (plane * TILE_DEV + tile) * PER_GRP + order
    all_keys = jnp.arange(PLANES * TILE_DEV * PER_GRP, dtype=jnp.int32)
    picked = jnp.sum(jnp.where(key[None, :] == all_keys[:, None], slot[None, :], 0), axis=1)
    return wanted, picked.reshape(PLANES, TILE_DEV * PER_GRP)


def kernel(
    asked, picked, q_ref, k_hbm, v_hbm, out_ref,
    pages_k, pages_v, r0, r1, r2, r3, r4, r5, r6, r7,
    stage, q_far, scores, probs, v_turned, own, part0, part1, part2, part_far,
    load_sem, send_sem, recv_sem, q_send, q_recv, part_send, part_recv,
):
    landed = (r0, r1, r2, r3, r4, r5, r6, r7)
    parts = (part0, part1, part2, own)
    g, c = lax.axis_index("grp"), lax.axis_index("ctx")
    x, y, core = c // 8, (c // 2) % 4, c % 2

    loads = [
        pltpu.make_async_copy(k_hbm, pages_k, load_sem.at[0]),
        pltpu.make_async_copy(v_hbm, pages_v, load_sem.at[1]),
    ]
    loads[0].start()
    loads[1].start()

    def peer(i):
        m = i % 16
        a = m % 4
        b = (m // 4 + a) % 4
        return (((x + a) % 4) * 4 + (y + b) % 4) * 2 + (core + i // 16) % 2

    barrier = pltpu.get_barrier_semaphore()

    def greet(i, carry):
        pl.semaphore_signal(barrier, inc=1, device_id=(g, peer(i)), device_id_type=MESH)
        return carry

    lax.fori_loop(1, CTX, greet, 0)
    for step in (1, 2, 3):
        pl.semaphore_signal(barrier, inc=1, device_id=((g + step) % 4, c), device_id_type=MESH)
    pl.semaphore_wait(barrier, PEERS + 3)

    q_copies = []
    for p in range(3):
        q_copies.append(
            pltpu.make_async_remote_copy(
                src_ref=q_ref,
                dst_ref=q_far.at[p],
                send_sem=q_send.at[p],
                recv_sem=q_recv.at[p],
                device_id=((g + 4 - PLANE_STEPS[p]) % 4, c),
                device_id_type=MESH,
            )
        )
        q_copies[-1].start()

    def copy_of(sp, i):
        w = (sp * PEERS + i - 1) % WINDOW
        return pltpu.make_async_remote_copy(
            src_ref=stage.at[w],
            dst_ref=landed[sp].at[pl.ds(c * CAP, CAP)],
            send_sem=send_sem.at[w],
            recv_sem=recv_sem.at[sp],
            device_id=(g, peer(i)),
            device_id_type=MESH,
        )

    def first_of(sp, i):
        return ((g + PLANE_STEPS[sp // 2]) % 4) * (CTX * CAP) + peer(i) * CAP

    def push(sp, i):
        pages = (pages_k, pages_v)[sp % 2]
        number = sp * PEERS + i - 1

        @pl.when(number >= WINDOW)
        def _():
            copy_of(sp, i).wait_send()

        w, first = number % WINDOW, first_of(sp, i)
        for r in range(CAP):
            stage[w, r] = pages[asked[first + r]]
        copy_of(sp, i).start()

    def keep(sp):
        pages = (pages_k, pages_v)[sp % 2]
        for r in range(CAP):
            landed[sp][c * CAP + r] = pages[asked[first_of(sp, 0) + r]]

    def push_range(sp, low, high):
        def one(i, carry):
            push(sp, i)
            return carry

        lax.fori_loop(low, high, one, 0)

    def push_some(sp, it):
        if sp + 1 >= 8:
            return

        def one(j, carry):
            n = it * 3 + j

            @pl.when(n < PEERS - AHEAD)
            def _():
                push(sp + 1, AHEAD + 1 + n)

            if sp + 2 < 8:

                @pl.when((n >= PEERS - AHEAD) & (n < PEERS))
                def _():
                    push(sp + 2, n - (PEERS - AHEAD) + 1)

            return carry

        lax.fori_loop(0, 3, one, 0)

    def arrived(sp):
        everything = landed[sp].at[pl.ds(0, PEERS * CAP)]
        pltpu.make_async_copy(everything, everything, recv_sem.at[sp]).wait()

    def score(p, it):
        t, pair = it // PAIRS, it % PAIRS
        rows = pl.ds(pl.multiple_of(t * BLOCK, BLOCK), BLOCK)
        columns = pl.ds(pl.multiple_of(pair * PAIR, PAIR), PAIR)
        both = q_far[p, rows, columns] if p < 3 else q_ref[rows, columns]
        queries = jnp.concatenate([both[:, :HD], both[:, HD:]], axis=0)
        base = ((g + PLANE_STEPS[p]) % 4) * (TILE_DEV * PER_GRP) + t * PER_GRP
        top = jnp.full((8, PAIR), -jnp.inf, jnp.float32)
        for j in range(PER_GRP):
            keys = landed[2 * p][picked[base + j]]
            s = lax.dot_general(keys, queries, (((1,), (1,)), ((), ())), preferred_element_type=jnp.float32)
            scores[j * BLOCK : (j + 1) * BLOCK, :] = s
            top = jnp.maximum(top, jnp.max(s.reshape(BLOCK // 8, 8, PAIR), axis=0))
        largest = jnp.max(top, axis=0, keepdims=True)
        total = jnp.zeros((8, PAIR), jnp.float32)
        for j in range(PER_GRP):
            w = jnp.exp2((scores[j * BLOCK : (j + 1) * BLOCK, :] - largest) * SCALE2)
            total = total + jnp.sum(w.reshape(BLOCK // 8, 8, PAIR), axis=0)
            probs[t, j * BLOCK : (j + 1) * BLOCK, columns] = w.astype(jnp.bfloat16)
        denominator = jnp.sum(total, axis=0, keepdims=True)
        upper = lax.broadcasted_iota(jnp.int32, (8, PAIR), 0) < 4
        parts[p][t, BLOCK:STATS, columns] = jnp.where(upper, largest, denominator)

    def turn(p, t):
        base = ((g + PLANE_STEPS[p]) % 4) * (TILE_DEV * PER_GRP) + t * PER_GRP
        for j in range(PER_GRP):
            values = landed[2 * p + 1][picked[base + j]].astype(jnp.float32)
            v_turned[:, j * BLOCK : (j + 1) * BLOCK] = values.T.astype(jnp.bfloat16)

    def weigh(p, it):
        t, pair = it // PAIRS, it % PAIRS
        columns = pl.ds(pl.multiple_of(pair * PAIR, PAIR), PAIR)

        @pl.when(pair == 0)
        def _():
            turn(p, t)

        parts[p][t, 0:BLOCK, columns] = jnp.dot(
            v_turned[...], probs[t, :, columns], preferred_element_type=jnp.float32
        )

    part_copies = []
    for p in range(3):
        part_copies.append(
            pltpu.make_async_remote_copy(
                src_ref=parts[p],
                dst_ref=part_far.at[p],
                send_sem=part_send.at[p],
                recv_sem=part_recv.at[p],
                device_id=((g + PLANE_STEPS[p]) % 4, c),
                device_id_type=MESH,
            )
        )

    loads[0].wait()
    keep(0)
    push_range(0, 1, CTX)
    loads[1].wait()
    keep(1)
    push_range(1, 1, AHEAD + 1)
    for p in range(4):
        for half in range(2):
            sp = 2 * p + half
            if sp + 2 < 8:
                keep(sp + 2)
            arrived(sp)
            if half == 0 and p < 3:
                q_copies[p].wait_recv()

            def work(it, carry, sp=sp, p=p, half=half):
                push_some(sp, it)
                (score if half == 0 else weigh)(p, it)
                return carry

            lax.fori_loop(0, ITEMS, work, 0)
        if p < 3:
            part_copies[p].start()

    for p in range(3):
        q_copies[p].wait_send()
        part_copies[p].wait_send()
        part_copies[p].wait_recv()

    def drain(w, carry):
        copy_of(0, w + 1).wait_send()
        return carry

    lax.fori_loop(0, WINDOW, drain, 0)

    def finish(it, carry):
        t, pair = it // PAIRS, it % PAIRS
        columns = pl.ds(pl.multiple_of(pair * PAIR, PAIR), PAIR)
        tops = [own[t, BLOCK : BLOCK + 1, columns]] + [part_far[p, t, BLOCK : BLOCK + 1, columns] for p in range(3)]
        sums = [own[t, BLOCK + 4 : BLOCK + 5, columns]] + [
            part_far[p, t, BLOCK + 4 : BLOCK + 5, columns] for p in range(3)
        ]
        largest = functools.reduce(jnp.maximum, tops)
        fades = [jnp.exp2((top - largest) * SCALE2) for top in tops]
        denominator = sum(f * s for f, s in zip(fades, sums, strict=True))
        summed = own[t, 0:BLOCK, columns] * fades[0]
        for p in range(3):
            summed = summed + part_far[p, t, 0:BLOCK, columns] * fades[p + 1]
        summed = summed / denominator
        rows = pl.ds(pl.multiple_of(t * BLOCK, BLOCK), BLOCK)
        out_ref[rows, columns] = jnp.concatenate([summed[:, :HD].T, summed[:, HD:].T], axis=1).astype(jnp.bfloat16)
        return carry

    lax.fori_loop(0, ITEMS, finish, 0)


def on_device(queries, keys_cache, values_cache, block_list, page_table):
    wanted, picked = request_plan(page_table[block_list])
    message = jnp.concatenate(
        [wanted, jnp.repeat(picked, CTX, axis=0)], axis=1
    )
    heard = lax.all_to_all(message[:, None, :], ("grp", "ctx"), split_axis=0, concat_axis=0, tiled=True)[:, 0]
    asked = heard[:, :CAP].reshape(-1)
    places = lax.dynamic_index_in_dim(
        heard[:, CAP:].reshape(PLANES, CTX, TILE_DEV * PER_GRP), lax.axis_index("ctx"), axis=1, keepdims=False
    ).reshape(-1)
    vmem, smem = pl.BlockSpec(memory_space=pltpu.VMEM), pl.BlockSpec(memory_space=pltpu.SMEM)
    whole = pl.BlockSpec(memory_space=pl.ANY)
    half_part = pltpu.VMEM((TILE_DEV, STATS, ROWS), jnp.float32)
    return pl.pallas_call(
        kernel,
        out_shape=jax.ShapeDtypeStruct((TILE_DEV * BLOCK, ROWS), jnp.bfloat16),
        in_specs=[smem, smem, vmem, whole, whole],
        out_specs=vmem,
        scratch_shapes=[
            pltpu.VMEM((BLK_DEV, BLOCK, HD), jnp.bfloat16),
            pltpu.VMEM((BLK_DEV, BLOCK, HD), jnp.bfloat16),
            *[pltpu.VMEM((CTX * CAP, BLOCK, HD), jnp.bfloat16)] * 8,
            pltpu.VMEM((WINDOW, CAP, BLOCK, HD), jnp.bfloat16),
            pltpu.VMEM((3, TILE_DEV * BLOCK, ROWS), jnp.bfloat16),
            pltpu.VMEM((KEYS, PAIR), jnp.float32),
            pltpu.VMEM((TILE_DEV, KEYS, ROWS), jnp.bfloat16),
            pltpu.VMEM((HD, KEYS), jnp.bfloat16),
            half_part,
            half_part,
            half_part,
            half_part,
            pltpu.VMEM((3, TILE_DEV, STATS, ROWS), jnp.float32),
            pltpu.SemaphoreType.DMA((2,)),
            pltpu.SemaphoreType.DMA((WINDOW,)),
            pltpu.SemaphoreType.DMA((8,)),
            pltpu.SemaphoreType.DMA((3,)),
            pltpu.SemaphoreType.DMA((3,)),
            pltpu.SemaphoreType.DMA((3,)),
            pltpu.SemaphoreType.DMA((3,)),
        ],
        compiler_params=pltpu.CompilerParams(
            collective_id=0, has_side_effects=True, vmem_limit_bytes=66_000_000
        ),
    )(asked, places, queries, keys_cache, values_cache)


def solution(mesh):
    in_specs = (
        P(("grp", "ctx"), None),
        P(("grp", "ctx"), None, None),
        P(("grp", "ctx"), None, None),
        P(("grp", "ctx"), None),
        P(),
    )
    return jax.shard_map(
        on_device, mesh=mesh, in_specs=in_specs, out_specs=P(("grp", "ctx"), None), check_vma=False
    )
```

```python
import functools
import math

import jax
import jax.numpy as jnp
from jax import lax
from jax.experimental import pallas as pl
from jax.experimental.pallas import tpu as pltpu
from jax.sharding import PartitionSpec as P

HD = 128
HEADS = 8
BLOCK = 128
NB = 36
TILE_DEV = 3
BLK_DEV = 128
CAP = 3
PLANES = 4
CTX = 32
PER_GRP = NB // PLANES
KEYS = PER_GRP * BLOCK
ROWS = HEADS * BLOCK
PAIR = 2 * BLOCK
PAIRS = ROWS // PAIR
ITEMS = TILE_DEV * PAIRS
WINDOW = 16
AHEAD = 15
PEERS = CTX - 1
PLANE_STEPS = (1, 3, 2, 0)
STATS = BLOCK + 8
MESH = pl.DeviceIdType.MESH
SCALE2 = HD**-0.5 * math.log2(math.e)


def request_plan(page_ids):
    flat = page_ids.reshape(-1)
    device_of, within = flat // BLK_DEV, flat % BLK_DEV
    position = jnp.arange(flat.shape[0], dtype=jnp.int32)
    earlier = position[None, :] < position[:, None]
    rank = jnp.sum(((device_of[None, :] == device_of[:, None]) & earlier).astype(jnp.int32), axis=1)
    devices = jnp.arange(PLANES * CTX, dtype=jnp.int32)
    ranks = jnp.arange(CAP, dtype=jnp.int32)
    place = (device_of * CAP + rank)[None, None, :] == (devices[:, None] * CAP + ranks)[:, :, None]
    wanted = jnp.sum(jnp.where(place, within[None, None, :], 0), axis=2)
    tile = position // NB
    plane = device_of // CTX
    same = (plane[None, :] == plane[:, None]) & (tile[None, :] == tile[:, None]) & earlier
    order = jnp.sum(same.astype(jnp.int32), axis=1)
    slot = (device_of % CTX) * CAP + rank
    key = (plane * TILE_DEV + tile) * PER_GRP + order
    all_keys = jnp.arange(PLANES * TILE_DEV * PER_GRP, dtype=jnp.int32)
    picked = jnp.sum(jnp.where(key[None, :] == all_keys[:, None], slot[None, :], 0), axis=1)
    return wanted, picked.reshape(PLANES, TILE_DEV * PER_GRP)


def kernel(
    asked, picked, q_ref, k_hbm, v_hbm, out_ref,
    pages_k, pages_v, r0, r1, r2, r3, r4, r5, r6, r7,
    stage, q_far, scores, probs, v_turned, own, part0, part1, part2, part_far,
    load_sem, send_sem, recv_sem, q_send, q_recv, part_send, part_recv,
):
    landed = (r0, r1, r2, r3, r4, r5, r6, r7)
    parts = (part0, part1, part2, own)
    g, c = lax.axis_index("grp"), lax.axis_index("ctx")
    x, y, core = c // 8, (c // 2) % 4, c % 2

    loads = [
        pltpu.make_async_copy(k_hbm, pages_k, load_sem.at[0]),
        pltpu.make_async_copy(v_hbm, pages_v, load_sem.at[1]),
    ]
    loads[0].start()
    loads[1].start()

    def walk(n):
        return (1 + 2 * n + n // 2) % 4

    def peer(i):
        far = i // 16
        m = (i + 15 + far) % 16
        a, b = walk(m % 4), walk(m // 4)
        b = b * (1 + 2 * (a // 3)) % 4
        moves = (a + 3) // 4
        b = (b + 2 * core * (moves + (1 - moves) * (b % 2))) % 4
        return (((x + a) % 4) * 4 + (y + b) % 4) * 2 + (core + far) % 2

    barrier = pltpu.get_barrier_semaphore()

    def greet(i, carry):
        pl.semaphore_signal(barrier, inc=1, device_id=(g, peer(i)), device_id_type=MESH)
        return carry

    lax.fori_loop(1, CTX, greet, 0)
    for step in (1, 2, 3):
        pl.semaphore_signal(barrier, inc=1, device_id=((g + step) % 4, c), device_id_type=MESH)
    pl.semaphore_wait(barrier, PEERS + 3)

    q_copies = []
    for p in range(3):
        q_copies.append(
            pltpu.make_async_remote_copy(
                src_ref=q_ref,
                dst_ref=q_far.at[p],
                send_sem=q_send.at[p],
                recv_sem=q_recv.at[p],
                device_id=((g + 4 - PLANE_STEPS[p]) % 4, c),
                device_id_type=MESH,
            )
        )
        q_copies[-1].start()

    def copy_of(sp, i):
        w = (sp * PEERS + i - 1) % WINDOW
        return pltpu.make_async_remote_copy(
            src_ref=stage.at[w],
            dst_ref=landed[sp].at[pl.ds(c * CAP, CAP)],
            send_sem=send_sem.at[w],
            recv_sem=recv_sem.at[sp],
            device_id=(g, peer(i)),
            device_id_type=MESH,
        )

    def first_of(sp, i):
        return ((g + PLANE_STEPS[sp // 2]) % 4) * (CTX * CAP) + peer(i) * CAP

    def push(sp, i):
        pages = (pages_k, pages_v)[sp % 2]
        number = sp * PEERS + i - 1

        @pl.when(number >= WINDOW)
        def _():
            copy_of(sp, i).wait_send()

        w, first = number % WINDOW, first_of(sp, i)
        for r in range(CAP):
            stage[w, r] = pages[asked[first + r]]
        copy_of(sp, i).start()

    def keep(sp):
        pages = (pages_k, pages_v)[sp % 2]
        for r in range(CAP):
            landed[sp][c * CAP + r] = pages[asked[first_of(sp, 0) + r]]

    def push_range(sp, low, high):
        def one(i, carry):
            push(sp, i)
            return carry

        lax.fori_loop(low, high, one, 0)

    def push_some(sp, it):
        if sp + 1 >= 8:
            return

        def one(j, carry):
            n = it * 3 + j

            @pl.when(n < PEERS - AHEAD)
            def _():
                push(sp + 1, AHEAD + 1 + n)

            if sp + 2 < 8:

                @pl.when((n >= PEERS - AHEAD) & (n < PEERS))
                def _():
                    push(sp + 2, n - (PEERS - AHEAD) + 1)

            return carry

        lax.fori_loop(0, 3, one, 0)

    def arrived(sp):
        everything = landed[sp].at[pl.ds(0, PEERS * CAP)]
        pltpu.make_async_copy(everything, everything, recv_sem.at[sp]).wait()

    def score(p, it):
        t, pair = it // PAIRS, it % PAIRS
        rows = pl.ds(pl.multiple_of(t * BLOCK, BLOCK), BLOCK)
        columns = pl.ds(pl.multiple_of(pair * PAIR, PAIR), PAIR)
        both = q_far[p, rows, columns] if p < 3 else q_ref[rows, columns]
        queries = jnp.concatenate([both[:, :HD], both[:, HD:]], axis=0)
        base = ((g + PLANE_STEPS[p]) % 4) * (TILE_DEV * PER_GRP) + t * PER_GRP
        top = jnp.full((8, PAIR), -jnp.inf, jnp.float32)
        for j in range(PER_GRP):
            keys = landed[2 * p][picked[base + j]]
            s = lax.dot_general(keys, queries, (((1,), (1,)), ((), ())), preferred_element_type=jnp.float32)
            scores[j * BLOCK : (j + 1) * BLOCK, :] = s
            top = jnp.maximum(top, jnp.max(s.reshape(BLOCK // 8, 8, PAIR), axis=0))
        largest = jnp.max(top, axis=0, keepdims=True)
        total = jnp.zeros((8, PAIR), jnp.float32)
        for j in range(PER_GRP):
            w = jnp.exp2((scores[j * BLOCK : (j + 1) * BLOCK, :] - largest) * SCALE2)
            total = total + jnp.sum(w.reshape(BLOCK // 8, 8, PAIR), axis=0)
            probs[t, j * BLOCK : (j + 1) * BLOCK, columns] = w.astype(jnp.bfloat16)
        denominator = jnp.sum(total, axis=0, keepdims=True)
        upper = lax.broadcasted_iota(jnp.int32, (8, PAIR), 0) < 4
        parts[p][t, BLOCK:STATS, columns] = jnp.where(upper, largest, denominator)

    def turn(p, t):
        base = ((g + PLANE_STEPS[p]) % 4) * (TILE_DEV * PER_GRP) + t * PER_GRP
        for j in range(PER_GRP):
            values = landed[2 * p + 1][picked[base + j]].astype(jnp.float32)
            v_turned[:, j * BLOCK : (j + 1) * BLOCK] = values.T.astype(jnp.bfloat16)

    def weigh(p, it):
        t, pair = it // PAIRS, it % PAIRS
        columns = pl.ds(pl.multiple_of(pair * PAIR, PAIR), PAIR)

        @pl.when(pair == 0)
        def _():
            turn(p, t)

        parts[p][t, 0:BLOCK, columns] = jnp.dot(
            v_turned[...], probs[t, :, columns], preferred_element_type=jnp.float32
        )

    part_copies = []
    for p in range(3):
        part_copies.append(
            pltpu.make_async_remote_copy(
                src_ref=parts[p],
                dst_ref=part_far.at[p],
                send_sem=part_send.at[p],
                recv_sem=part_recv.at[p],
                device_id=((g + PLANE_STEPS[p]) % 4, c),
                device_id_type=MESH,
            )
        )

    loads[0].wait()
    keep(0)
    push_range(0, 1, CTX)
    loads[1].wait()
    keep(1)
    push_range(1, 1, AHEAD + 1)
    for p in range(4):
        for half in range(2):
            sp = 2 * p + half
            if sp + 2 < 8:
                keep(sp + 2)
            arrived(sp)
            if half == 0 and p < 3:
                q_copies[p].wait_recv()

            def work(it, carry, sp=sp, p=p, half=half):
                push_some(sp, it)
                (score if half == 0 else weigh)(p, it)
                return carry

            lax.fori_loop(0, ITEMS, work, 0)
        if p < 3:
            part_copies[p].start()

    for p in range(3):
        q_copies[p].wait_send()
        part_copies[p].wait_send()
        part_copies[p].wait_recv()

    def drain(w, carry):
        copy_of(0, w + 1).wait_send()
        return carry

    lax.fori_loop(0, WINDOW, drain, 0)

    def finish(it, carry):
        t, pair = it // PAIRS, it % PAIRS
        columns = pl.ds(pl.multiple_of(pair * PAIR, PAIR), PAIR)
        tops = [own[t, BLOCK : BLOCK + 1, columns]] + [part_far[p, t, BLOCK : BLOCK + 1, columns] for p in range(3)]
        sums = [own[t, BLOCK + 4 : BLOCK + 5, columns]] + [
            part_far[p, t, BLOCK + 4 : BLOCK + 5, columns] for p in range(3)
        ]
        largest = functools.reduce(jnp.maximum, tops)
        fades = [jnp.exp2((top - largest) * SCALE2) for top in tops]
        denominator = sum(f * s for f, s in zip(fades, sums, strict=True))
        summed = own[t, 0:BLOCK, columns] * fades[0]
        for p in range(3):
            summed = summed + part_far[p, t, 0:BLOCK, columns] * fades[p + 1]
        summed = summed / denominator
        rows = pl.ds(pl.multiple_of(t * BLOCK, BLOCK), BLOCK)
        out_ref[rows, columns] = jnp.concatenate([summed[:, :HD].T, summed[:, HD:].T], axis=1).astype(jnp.bfloat16)
        return carry

    lax.fori_loop(0, ITEMS, finish, 0)


def on_device(queries, keys_cache, values_cache, block_list, page_table):
    wanted, picked = request_plan(page_table[block_list])
    message = jnp.concatenate(
        [wanted, jnp.repeat(picked, CTX, axis=0)], axis=1
    )
    heard = lax.all_to_all(message[:, None, :], ("grp", "ctx"), split_axis=0, concat_axis=0, tiled=True)[:, 0]
    asked = heard[:, :CAP].reshape(-1)
    places = lax.dynamic_index_in_dim(
        heard[:, CAP:].reshape(PLANES, CTX, TILE_DEV * PER_GRP), lax.axis_index("ctx"), axis=1, keepdims=False
    ).reshape(-1)
    vmem, smem = pl.BlockSpec(memory_space=pltpu.VMEM), pl.BlockSpec(memory_space=pltpu.SMEM)
    whole = pl.BlockSpec(memory_space=pl.ANY)
    half_part = pltpu.VMEM((TILE_DEV, STATS, ROWS), jnp.float32)
    return pl.pallas_call(
        kernel,
        out_shape=jax.ShapeDtypeStruct((TILE_DEV * BLOCK, ROWS), jnp.bfloat16),
        in_specs=[smem, smem, vmem, whole, whole],
        out_specs=vmem,
        scratch_shapes=[
            pltpu.VMEM((BLK_DEV, BLOCK, HD), jnp.bfloat16),
            pltpu.VMEM((BLK_DEV, BLOCK, HD), jnp.bfloat16),
            *[pltpu.VMEM((CTX * CAP, BLOCK, HD), jnp.bfloat16)] * 8,
            pltpu.VMEM((WINDOW, CAP, BLOCK, HD), jnp.bfloat16),
            pltpu.VMEM((3, TILE_DEV * BLOCK, ROWS), jnp.bfloat16),
            pltpu.VMEM((KEYS, PAIR), jnp.float32),
            pltpu.VMEM((TILE_DEV, KEYS, ROWS), jnp.bfloat16),
            pltpu.VMEM((HD, KEYS), jnp.bfloat16),
            half_part,
            half_part,
            half_part,
            half_part,
            pltpu.VMEM((3, TILE_DEV, STATS, ROWS), jnp.float32),
            pltpu.SemaphoreType.DMA((2,)),
            pltpu.SemaphoreType.DMA((WINDOW,)),
            pltpu.SemaphoreType.DMA((8,)),
            pltpu.SemaphoreType.DMA((3,)),
            pltpu.SemaphoreType.DMA((3,)),
            pltpu.SemaphoreType.DMA((3,)),
            pltpu.SemaphoreType.DMA((3,)),
        ],
        compiler_params=pltpu.CompilerParams(
            collective_id=0, has_side_effects=True, vmem_limit_bytes=66_000_000
        ),
    )(asked, places, queries, keys_cache, values_cache)


def solution(mesh):
    in_specs = (
        P(("grp", "ctx"), None),
        P(("grp", "ctx"), None, None),
        P(("grp", "ctx"), None, None),
        P(("grp", "ctx"), None),
        P(),
    )
    return jax.shard_map(
        on_device, mesh=mesh, in_specs=in_specs, out_specs=P(("grp", "ctx"), None), check_vma=False
    )
```

```python
import functools
import math

import jax
import jax.numpy as jnp
from jax import lax
from jax.experimental import pallas as pl
from jax.experimental.pallas import tpu as pltpu
from jax.sharding import PartitionSpec as P

HD = 128
HEADS = 8
BLOCK = 128
NB = 36
TILE_DEV = 3
BLK_DEV = 128
CAP = 3
PLANES = 4
CTX = 32
PER_GRP = NB // PLANES
KEYS = PER_GRP * BLOCK
ROWS = HEADS * BLOCK
PAIR = 2 * BLOCK
PAIRS = ROWS // PAIR
ITEMS = TILE_DEV * PAIRS
WINDOW = 16
AHEAD = 15
PEERS = CTX - 1
PLANE_STEPS = (1, 3, 2, 0)
STATS = BLOCK + 8
MESH = pl.DeviceIdType.MESH
SCALE2 = HD**-0.5 * math.log2(math.e)


def request_plan(page_ids):
    flat = page_ids.reshape(-1)
    device_of, within = flat // BLK_DEV, flat % BLK_DEV
    position = jnp.arange(flat.shape[0], dtype=jnp.int32)
    earlier = position[None, :] < position[:, None]
    rank = jnp.sum(((device_of[None, :] == device_of[:, None]) & earlier).astype(jnp.int32), axis=1)
    devices = jnp.arange(PLANES * CTX, dtype=jnp.int32)
    ranks = jnp.arange(CAP, dtype=jnp.int32)
    place = (device_of * CAP + rank)[None, None, :] == (devices[:, None] * CAP + ranks)[:, :, None]
    wanted = jnp.sum(jnp.where(place, within[None, None, :], 0), axis=2)
    tile = position // NB
    plane = device_of // CTX
    same = (plane[None, :] == plane[:, None]) & (tile[None, :] == tile[:, None]) & earlier
    order = jnp.sum(same.astype(jnp.int32), axis=1)
    slot = (device_of % CTX) * CAP + rank
    key = (plane * TILE_DEV + tile) * PER_GRP + order
    all_keys = jnp.arange(PLANES * TILE_DEV * PER_GRP, dtype=jnp.int32)
    picked = jnp.sum(jnp.where(key[None, :] == all_keys[:, None], slot[None, :], 0), axis=1)
    return wanted, picked.reshape(PLANES, TILE_DEV * PER_GRP)


def kernel(
    ask, q_ref, k_hbm, v_hbm, out_ref,
    pages_k, pages_v, r0, r1, r2, r3, r4, r5, r6, r7,
    stage, q_far, scores, probs, v_turned, own, part0, part1, part2, part_far,
    heard, told, asked, picked,
    load_sem, send_sem, recv_sem, q_send, q_recv, part_send, part_recv, ask_send, ask_recv, tell_sem, note_sem,
):
    landed = (r0, r1, r2, r3, r4, r5, r6, r7)
    parts = (part0, part1, part2, own)
    g, c = lax.axis_index("grp"), lax.axis_index("ctx")
    x, y, core = c // 8, (c // 2) % 4, c % 2

    loads = [
        pltpu.make_async_copy(k_hbm, pages_k, load_sem.at[0]),
        pltpu.make_async_copy(v_hbm, pages_v, load_sem.at[1]),
    ]
    loads[0].start()
    loads[1].start()

    def walk(n):
        return (1 + 2 * n + n // 2) % 4

    def peer(i):
        far = i // 16
        m = (i + 15 + far) % 16
        a, b = walk(m % 4), walk(m // 4)
        b = b * (1 + 2 * (a // 3)) % 4
        moves = (a + 3) // 4
        b = (b + 2 * core * (moves + (1 - moves) * (b % 2))) % 4
        return (((x + a) % 4) * 4 + (y + b) % 4) * 2 + (core + far) % 2

    barrier = pltpu.get_barrier_semaphore()

    def greet(i, carry):
        pl.semaphore_signal(barrier, inc=1, device_id=(g, peer(i)), device_id_type=MESH)
        return carry

    lax.fori_loop(1, CTX, greet, 0)
    for step in (1, 2, 3):
        pl.semaphore_signal(barrier, inc=1, device_id=((g + step) % 4, c), device_id_type=MESH)
    pl.semaphore_wait(barrier, PEERS + 3)

    asks = []
    for step in (1, 2, 3):
        asks.append(
            pltpu.make_async_remote_copy(
                src_ref=ask.at[(g + step) % 4],
                dst_ref=heard.at[g],
                send_sem=ask_send.at[step],
                recv_sem=ask_recv.at[step],
                device_id=((g + step) % 4, c),
                device_id_type=MESH,
            )
        )
        asks[-1].start()
    asks.append(pltpu.make_async_copy(ask.at[g], heard.at[g], ask_send.at[0]))
    asks[-1].start()
    for copy in asks:
        copy.wait()

    def tell(i, carry):
        pltpu.make_async_remote_copy(
            src_ref=heard.at[:, peer(i)],
            dst_ref=told.at[c],
            send_sem=tell_sem.at[0],
            recv_sem=tell_sem.at[1],
            device_id=(g, peer(i)),
            device_id_type=MESH,
        ).start()
        return carry

    lax.fori_loop(1, CTX, tell, 0)
    note = [
        pltpu.make_async_copy(heard.at[:, c], told.at[c], note_sem.at[0]),
        pltpu.make_async_copy(heard.at[:, CTX], picked, note_sem.at[1]),
    ]
    for copy in note:
        copy.start()
    for copy in note:
        copy.wait()
    for way in range(2):
        everyone = told.at[pl.ds(0, PEERS)]
        pltpu.make_async_copy(everyone, everyone, tell_sem.at[way]).wait()
    note = pltpu.make_async_copy(told, asked, note_sem.at[0])
    note.start()
    note.wait()

    q_copies = []
    for p in range(3):
        q_copies.append(
            pltpu.make_async_remote_copy(
                src_ref=q_ref,
                dst_ref=q_far.at[p],
                send_sem=q_send.at[p],
                recv_sem=q_recv.at[p],
                device_id=((g + 4 - PLANE_STEPS[p]) % 4, c),
                device_id_type=MESH,
            )
        )
        q_copies[-1].start()

    def copy_of(sp, i):
        w = (sp * PEERS + i - 1) % WINDOW
        return pltpu.make_async_remote_copy(
            src_ref=stage.at[w],
            dst_ref=landed[sp].at[pl.ds(c * CAP, CAP)],
            send_sem=send_sem.at[w],
            recv_sem=recv_sem.at[sp],
            device_id=(g, peer(i)),
            device_id_type=MESH,
        )

    def plane_of(p):
        return (g + PLANE_STEPS[p]) % 4

    def push(sp, i):
        pages = (pages_k, pages_v)[sp % 2]
        number = sp * PEERS + i - 1

        @pl.when(number >= WINDOW)
        def _():
            copy_of(sp, i).wait_send()

        w, who = number % WINDOW, peer(i)
        for r in range(CAP):
            stage[w, r] = pages[asked[who, plane_of(sp // 2), 0, r]]
        copy_of(sp, i).start()

    def keep(sp):
        pages = (pages_k, pages_v)[sp % 2]
        for r in range(CAP):
            landed[sp][c * CAP + r] = pages[asked[c, plane_of(sp // 2), 0, r]]

    def push_range(sp, low, high):
        def one(i, carry):
            push(sp, i)
            return carry

        lax.fori_loop(low, high, one, 0)

    def push_some(sp, it):
        if sp + 1 >= 8:
            return

        def one(j, carry):
            n = it * 3 + j

            @pl.when(n < PEERS - AHEAD)
            def _():
                push(sp + 1, AHEAD + 1 + n)

            if sp + 2 < 8:

                @pl.when((n >= PEERS - AHEAD) & (n < PEERS))
                def _():
                    push(sp + 2, n - (PEERS - AHEAD) + 1)

            return carry

        lax.fori_loop(0, 3, one, 0)

    def arrived(sp):
        everything = landed[sp].at[pl.ds(0, PEERS * CAP)]
        pltpu.make_async_copy(everything, everything, recv_sem.at[sp]).wait()

    def score(p, it):
        t, pair = it // PAIRS, it % PAIRS
        rows = pl.ds(pl.multiple_of(t * BLOCK, BLOCK), BLOCK)
        columns = pl.ds(pl.multiple_of(pair * PAIR, PAIR), PAIR)
        both = q_far[p, rows, columns] if p < 3 else q_ref[rows, columns]
        queries = jnp.concatenate([both[:, :HD], both[:, HD:]], axis=0)
        top = jnp.full((8, PAIR), -jnp.inf, jnp.float32)
        for j in range(PER_GRP):
            keys = landed[2 * p][picked[plane_of(p), 0, t * PER_GRP + j]]
            s = lax.dot_general(keys, queries, (((1,), (1,)), ((), ())), preferred_element_type=jnp.float32)
            scores[j * BLOCK : (j + 1) * BLOCK, :] = s
            top = jnp.maximum(top, jnp.max(s.reshape(BLOCK // 8, 8, PAIR), axis=0))
        largest = jnp.max(top, axis=0, keepdims=True)
        total = jnp.zeros((8, PAIR), jnp.float32)
        for j in range(PER_GRP):
            w = jnp.exp2((scores[j * BLOCK : (j + 1) * BLOCK, :] - largest) * SCALE2)
            total = total + jnp.sum(w.reshape(BLOCK // 8, 8, PAIR), axis=0)
            probs[t, j * BLOCK : (j + 1) * BLOCK, columns] = w.astype(jnp.bfloat16)
        denominator = jnp.sum(total, axis=0, keepdims=True)
        upper = lax.broadcasted_iota(jnp.int32, (8, PAIR), 0) < 4
        parts[p][t, BLOCK:STATS, columns] = jnp.where(upper, largest, denominator)

    def gather_values(p, t):
        for j in range(PER_GRP):
            v_turned[:, j * BLOCK : (j + 1) * BLOCK] = landed[2 * p + 1][picked[plane_of(p), 0, t * PER_GRP + j]]

    def part_copy(p, t):
        return pltpu.make_async_remote_copy(
            src_ref=parts[p].at[t],
            dst_ref=part_far.at[p, t],
            send_sem=part_send.at[p, t],
            recv_sem=part_recv.at[p, t],
            device_id=(plane_of(p), c),
            device_id_type=MESH,
        )

    def weigh(p, it):
        t, pair = it // PAIRS, it % PAIRS
        columns = pl.ds(pl.multiple_of(pair * PAIR, PAIR), PAIR)

        @pl.when(pair == 0)
        def _():
            gather_values(p, t)

        summed = jnp.dot(v_turned[...], probs[t, :, columns], preferred_element_type=jnp.float32)
        if p < 3:
            parts[p][t, 0:BLOCK, columns] = summed

            @pl.when(pair == PAIRS - 1)
            def _():
                part_copy(p, t).start()
        else:
            result = summed * part_far[0, t, BLOCK : BLOCK + 1, columns] + part_far[0, t, 0:BLOCK, columns]
            rows = pl.ds(pl.multiple_of(t * BLOCK, BLOCK), BLOCK)
            out_ref[rows, columns] = jnp.concatenate([result[:, :HD].T, result[:, HD:].T], axis=1).astype(jnp.bfloat16)

    def settle(it, carry):
        t, pair = it // PAIRS, it % PAIRS
        columns = pl.ds(pl.multiple_of(pair * PAIR, PAIR), PAIR)
        stats = [own[t, BLOCK:STATS, columns]] + [part_far[p, t, BLOCK:STATS, columns] for p in range(3)]
        tops, sums = [v[0:1] for v in stats], [v[4:5] for v in stats]
        largest = functools.reduce(jnp.maximum, tops)
        fades = [jnp.exp2((top - largest) * SCALE2) for top in tops]
        denominator = sum(f * v for f, v in zip(fades, sums, strict=True))
        fades = [f / denominator for f in fades]
        rest = part_far[0, t, 0:BLOCK, columns] * fades[1]
        for p in (1, 2):
            rest = rest + part_far[p, t, 0:BLOCK, columns] * fades[p + 1]
        part_far[0, t, 0:BLOCK, columns] = rest
        part_far[0, t, BLOCK:STATS, columns] = jnp.broadcast_to(fades[0], (8, PAIR))
        return carry

    loads[0].wait()
    keep(0)
    push_range(0, 1, WINDOW + 1)
    loads[1].wait()

    def turn(i):
        pages_v[i] = pages_v[i].astype(jnp.float32).T.astype(jnp.bfloat16)

    def push_and_turn(i, carry):
        push(0, i)
        for n in range(8):
            turn((i - WINDOW - 1) * 8 + n)
        return carry

    lax.fori_loop(WINDOW + 1, CTX, push_and_turn, 0)
    for n in range((PEERS - WINDOW) * 8, BLK_DEV):
        turn(n)
    keep(1)
    push_range(1, 1, AHEAD + 1)
    for p in range(4):
        for half in range(2):
            sp = 2 * p + half
            if sp + 2 < 8:
                keep(sp + 2)
            if sp == 7:
                for far in range(3):
                    for t in range(TILE_DEV):
                        part_copy(far, t).wait_recv()
                lax.fori_loop(0, ITEMS, settle, 0)
            arrived(sp)
            if half == 0 and p < 3:
                q_copies[p].wait_recv()

            def work(it, carry, sp=sp, p=p, half=half):
                push_some(sp, it)
                (score if half == 0 else weigh)(p, it)
                return carry

            lax.fori_loop(0, ITEMS, work, 0)

    for p in range(3):
        q_copies[p].wait_send()
        for t in range(TILE_DEV):
            part_copy(p, t).wait_send()

    def drain(w, carry):
        copy_of(0, w + 1).wait_send()
        return carry

    lax.fori_loop(0, WINDOW, drain, 0)


def on_device(queries, keys_cache, values_cache, block_list, page_table):
    wanted, picked = request_plan(page_table[block_list])
    lanes = BLOCK
    ask = jnp.concatenate(
        [
            jnp.pad(wanted, ((0, 0), (0, lanes - CAP))).reshape(PLANES, CTX, lanes),
            jnp.pad(picked, ((0, 0), (0, lanes - TILE_DEV * PER_GRP)))[:, None],
        ],
        axis=1,
    )[:, :, None]
    vmem = pl.BlockSpec(memory_space=pltpu.VMEM)
    whole = pl.BlockSpec(memory_space=pl.ANY)
    half_part = pltpu.VMEM((TILE_DEV, STATS, ROWS), jnp.float32)
    return pl.pallas_call(
        kernel,
        out_shape=jax.ShapeDtypeStruct((TILE_DEV * BLOCK, ROWS), jnp.bfloat16),
        in_specs=[vmem, vmem, whole, whole],
        out_specs=vmem,
        scratch_shapes=[
            pltpu.VMEM((BLK_DEV, BLOCK, HD), jnp.bfloat16),
            pltpu.VMEM((BLK_DEV, BLOCK, HD), jnp.bfloat16),
            *[pltpu.VMEM((CTX * CAP, BLOCK, HD), jnp.bfloat16)] * 8,
            pltpu.VMEM((WINDOW, CAP, BLOCK, HD), jnp.bfloat16),
            pltpu.VMEM((3, TILE_DEV * BLOCK, ROWS), jnp.bfloat16),
            pltpu.VMEM((KEYS, PAIR), jnp.float32),
            pltpu.VMEM((TILE_DEV, KEYS, ROWS), jnp.bfloat16),
            pltpu.VMEM((HD, KEYS), jnp.bfloat16),
            half_part,
            half_part,
            half_part,
            half_part,
            pltpu.VMEM((3, TILE_DEV, STATS, ROWS), jnp.float32),
            pltpu.VMEM((PLANES, CTX + 1, 1, BLOCK), jnp.int32),
            pltpu.VMEM((CTX, PLANES, 1, BLOCK), jnp.int32),
            pltpu.SMEM((CTX, PLANES, 1, BLOCK), jnp.int32),
            pltpu.SMEM((PLANES, 1, BLOCK), jnp.int32),
            pltpu.SemaphoreType.DMA((2,)),
            pltpu.SemaphoreType.DMA((WINDOW,)),
            pltpu.SemaphoreType.DMA((8,)),
            pltpu.SemaphoreType.DMA((3,)),
            pltpu.SemaphoreType.DMA((3,)),
            pltpu.SemaphoreType.DMA((3, TILE_DEV)),
            pltpu.SemaphoreType.DMA((3, TILE_DEV)),
            pltpu.SemaphoreType.DMA((4,)),
            pltpu.SemaphoreType.DMA((4,)),
            pltpu.SemaphoreType.DMA((2,)),
            pltpu.SemaphoreType.DMA((2,)),
        ],
        compiler_params=pltpu.CompilerParams(
            collective_id=0, has_side_effects=True, vmem_limit_bytes=66_000_000
        ),
    )(ask, queries, keys_cache, values_cache)


def solution(mesh):
    in_specs = (
        P(("grp", "ctx"), None),
        P(("grp", "ctx"), None, None),
        P(("grp", "ctx"), None, None),
        P(("grp", "ctx"), None),
        P(),
    )
    return jax.shard_map(
        on_device, mesh=mesh, in_specs=in_specs, out_specs=P(("grp", "ctx"), None), check_vma=False
    )
```

```python
import functools
import math

import jax
import jax.numpy as jnp
from jax import lax
from jax.experimental import pallas as pl
from jax.experimental.pallas import tpu as pltpu
from jax.sharding import PartitionSpec as P

HD = 128
HEADS = 8
BLOCK = 128
NB = 36
TILE_DEV = 3
BLK_DEV = 128
CAP = 3
PLANES = 4
CTX = 32
PER_GRP = NB // PLANES
KEYS = PER_GRP * BLOCK
ROWS = HEADS * BLOCK
PAIR = 2 * BLOCK
PAIRS = ROWS // PAIR
ITEMS = TILE_DEV * PAIRS
WINDOW = 16
AHEAD = 15
EARLY = 12
OWN_KEYS = 6
FIRST = WINDOW - EARLY + 1
TURNS = BLK_DEV // (32 - FIRST)
PEERS = CTX - 1
PLANE_STEPS = (1, 3, 2, 0)
STATS = BLOCK + 8
MESH = pl.DeviceIdType.MESH
SCALE2 = HD**-0.5 * math.log2(math.e)


def request_plan(page_ids):
    flat = page_ids.reshape(-1)
    device_of, within = flat // BLK_DEV, flat % BLK_DEV
    position = jnp.arange(flat.shape[0], dtype=jnp.int32)
    earlier = position[None, :] < position[:, None]
    rank = jnp.sum(((device_of[None, :] == device_of[:, None]) & earlier).astype(jnp.int32), axis=1)
    devices = jnp.arange(PLANES * CTX, dtype=jnp.int32)
    ranks = jnp.arange(CAP, dtype=jnp.int32)
    place = (device_of * CAP + rank)[None, None, :] == (devices[:, None] * CAP + ranks)[:, :, None]
    wanted = jnp.sum(jnp.where(place, within[None, None, :], 0), axis=2)
    tile = position // NB
    plane = device_of // CTX
    same = (plane[None, :] == plane[:, None]) & (tile[None, :] == tile[:, None]) & earlier
    order = jnp.sum(same.astype(jnp.int32), axis=1)
    slot = (device_of % CTX) * CAP + rank
    key = (plane * TILE_DEV + tile) * PER_GRP + order
    all_keys = jnp.arange(PLANES * TILE_DEV * PER_GRP, dtype=jnp.int32)
    picked = jnp.sum(jnp.where(key[None, :] == all_keys[:, None], slot[None, :], 0), axis=1)
    return wanted, picked.reshape(PLANES, TILE_DEV * PER_GRP)


def kernel(
    ask, q_hbm, k_hbm, v_hbm, out_ref,
    q_ref, near, near_asked,
    pages_k, pages_v, r0, r1, r2, r3, r4, r5, r6, r7,
    stage, q_far, scores, probs, v_turned, own, part0, part1, part2, part_far,
    heard, told, asked, picked,
    load_sem, send_sem, recv_sem, q_send, q_recv, part_send, part_recv, ask_send, ask_recv, tell_sem, near_sem, note_sem,
):
    landed = (r0, r1, r2, r3, r4, r5, r6, r7)
    parts = (part0, part1, part2, own)
    g, c = lax.axis_index("grp"), lax.axis_index("ctx")
    x, y, core = c // 8, (c // 2) % 4, c % 2

    loads = [
        pltpu.make_async_copy(k_hbm, pages_k, load_sem.at[0]),
        pltpu.make_async_copy(v_hbm, pages_v, load_sem.at[1]),
        pltpu.make_async_copy(q_hbm, q_ref, load_sem.at[2]),
    ]
    loads[0].start()
    loads[2].start()
    loads[1].start()

    def walk(n):
        return (1 + 2 * n + n // 2) % 4

    def peer(i):
        far = i // 16
        m = (i + 15 + far) % 16
        a, b = walk(m % 4), walk(m // 4)
        b = b * (1 + 2 * (a // 3)) % 4
        moves = (a + 3) // 4
        b = (b + 2 * core * (moves + (1 - moves) * (b % 2))) % 4
        return (((x + a) % 4) * 4 + (y + b) % 4) * 2 + (core + far) % 2

    barrier = pltpu.get_barrier_semaphore()

    def greet(i, carry):
        pl.semaphore_signal(barrier, inc=1, device_id=(g, peer(i)), device_id_type=MESH)
        return carry

    lax.fori_loop(1, CTX, greet, 0)
    for step in (1, 2, 3):
        pl.semaphore_signal(barrier, inc=1, device_id=((g + step) % 4, c), device_id_type=MESH)
    pl.semaphore_wait(barrier, PEERS + 3)

    def plane_of(p):
        return (g + PLANE_STEPS[p]) % 4

    def number_of(sp, i):
        return sp * PEERS + i - 1 + (EARLY if sp < OWN_KEYS else 0)

    def copy_of(sp, i, number):
        w = number % WINDOW
        return pltpu.make_async_remote_copy(
            src_ref=stage.at[w],
            dst_ref=landed[sp].at[pl.ds(c * CAP, CAP)],
            send_sem=send_sem.at[w],
            recv_sem=recv_sem.at[sp],
            device_id=(g, peer(i)),
            device_id_type=MESH,
        )

    def push(sp, i):
        pages = (pages_k, pages_v)[sp % 2]
        number = number_of(sp, i)

        @pl.when(number >= WINDOW)
        def _():
            copy_of(sp, i, number).wait_send()

        w, who = number % WINDOW, peer(i)
        for r in range(CAP):
            stage[w, r] = pages[asked[who, plane_of(sp // 2), 0, r]]
        copy_of(sp, i, number).start()

    def push_early(i, carry):
        who = peer(i)
        for r in range(CAP):
            stage[i - 1, r] = pages_k[near_asked[who, 0, r]]
        copy_of(OWN_KEYS, i, i - 1).start()
        return carry

    asks = []
    for step in (1, 2, 3):
        asks.append(
            pltpu.make_async_remote_copy(
                src_ref=ask.at[(g + step) % 4],
                dst_ref=heard.at[g],
                send_sem=ask_send.at[step],
                recv_sem=ask_recv.at[step],
                device_id=((g + step) % 4, c),
                device_id_type=MESH,
            )
        )
        asks[-1].start()
    asks.append(pltpu.make_async_copy(ask.at[g], heard.at[g], ask_send.at[0]))
    asks[-1].start()

    def tell_near(i, carry):
        pltpu.make_async_remote_copy(
            src_ref=ask.at[g, peer(i)],
            dst_ref=near.at[c],
            send_sem=near_sem.at[0],
            recv_sem=near_sem.at[1],
            device_id=(g, peer(i)),
            device_id_type=MESH,
        ).start()
        return carry

    own_near = pltpu.make_async_copy(ask.at[g, c], near.at[c], near_sem.at[2])
    own_near.start()
    lax.fori_loop(1, CTX, tell_near, 0)
    for copy in asks:
        copy.wait()

    def tell(i, carry):
        pltpu.make_async_remote_copy(
            src_ref=heard.at[:, peer(i)],
            dst_ref=told.at[c],
            send_sem=tell_sem.at[0],
            recv_sem=tell_sem.at[1],
            device_id=(g, peer(i)),
            device_id_type=MESH,
        ).start()
        return carry

    lax.fori_loop(1, CTX, tell, 0)
    own_list = pltpu.make_async_copy(heard.at[:, c], told.at[c], note_sem.at[0])
    own_picks = pltpu.make_async_copy(heard.at[:, CTX], picked, note_sem.at[1])
    own_list.start()
    own_picks.start()
    for way in range(2):
        everyone = near.at[pl.ds(0, PEERS)]
        pltpu.make_async_copy(everyone, everyone, near_sem.at[way]).wait()
    own_near.wait()
    near_note = pltpu.make_async_copy(near, near_asked, near_sem.at[2])
    near_note.start()
    near_note.wait()
    loads[0].wait()
    lax.fori_loop(1, EARLY + 1, push_early, 0)

    loads[2].wait()

    q_copies = []
    for p in range(3):
        q_copies.append(
            pltpu.make_async_remote_copy(
                src_ref=q_ref,
                dst_ref=q_far.at[p],
                send_sem=q_send.at[p],
                recv_sem=q_recv.at[p],
                device_id=((g + 4 - PLANE_STEPS[p]) % 4, c),
                device_id_type=MESH,
            )
        )
        q_copies[-1].start()

    own_list.wait()
    own_picks.wait()
    for way in range(2):
        everyone = told.at[pl.ds(0, PEERS)]
        pltpu.make_async_copy(everyone, everyone, tell_sem.at[way]).wait()
    note = pltpu.make_async_copy(told, asked, note_sem.at[0])
    note.start()
    note.wait()

    def keep(sp):
        pages = (pages_k, pages_v)[sp % 2]
        for r in range(CAP):
            landed[sp][c * CAP + r] = pages[asked[c, plane_of(sp // 2), 0, r]]

    def push_range(sp, low, high):
        def one(i, carry):
            push(sp, i)
            return carry

        lax.fori_loop(low, high, one, 0)

    def push_some(sp, it):
        if sp + 1 >= 8:
            return

        def one(j, carry):
            n = it * 3 + j

            @pl.when(n < PEERS - AHEAD)
            def _():
                push(sp + 1, AHEAD + 1 + n)

            if sp + 2 < 8:

                begun = EARLY if sp + 2 == OWN_KEYS else 0

                @pl.when((n >= PEERS - AHEAD + begun) & (n < PEERS))
                def _():
                    push(sp + 2, n - (PEERS - AHEAD) + 1)

            return carry

        lax.fori_loop(0, 3, one, 0)

    def arrived(sp):
        everything = landed[sp].at[pl.ds(0, PEERS * CAP)]
        pltpu.make_async_copy(everything, everything, recv_sem.at[sp]).wait()

    def score(p, it):
        t, pair = it // PAIRS, it % PAIRS
        rows = pl.ds(pl.multiple_of(t * BLOCK, BLOCK), BLOCK)
        columns = pl.ds(pl.multiple_of(pair * PAIR, PAIR), PAIR)
        both = q_far[p, rows, columns] if p < 3 else q_ref[rows, columns]
        queries = jnp.concatenate([both[:, :HD], both[:, HD:]], axis=0)
        top = jnp.full((8, PAIR), -jnp.inf, jnp.float32)
        for j in range(PER_GRP):
            keys = landed[2 * p][picked[plane_of(p), 0, t * PER_GRP + j]]
            s = lax.dot_general(keys, queries, (((1,), (1,)), ((), ())), preferred_element_type=jnp.float32)
            scores[j * BLOCK : (j + 1) * BLOCK, :] = s
            top = jnp.maximum(top, jnp.max(s.reshape(BLOCK // 8, 8, PAIR), axis=0))
        largest = jnp.max(top, axis=0, keepdims=True)
        total = jnp.zeros((8, PAIR), jnp.float32)
        for j in range(PER_GRP):
            w = jnp.exp2((scores[j * BLOCK : (j + 1) * BLOCK, :] - largest) * SCALE2)
            total = total + jnp.sum(w.reshape(BLOCK // 8, 8, PAIR), axis=0)
            probs[t, j * BLOCK : (j + 1) * BLOCK, columns] = w.astype(jnp.bfloat16)
        denominator = jnp.sum(total, axis=0, keepdims=True)
        upper = lax.broadcasted_iota(jnp.int32, (8, PAIR), 0) < 4
        parts[p][t, BLOCK:STATS, columns] = jnp.where(upper, largest, denominator)

    def gather_values(p, t):
        for j in range(PER_GRP):
            v_turned[:, j * BLOCK : (j + 1) * BLOCK] = landed[2 * p + 1][picked[plane_of(p), 0, t * PER_GRP + j]]

    def part_copy(p, t):
        return pltpu.make_async_remote_copy(
            src_ref=parts[p].at[t],
            dst_ref=part_far.at[p, t],
            send_sem=part_send.at[p, t],
            recv_sem=part_recv.at[p, t],
            device_id=(plane_of(p), c),
            device_id_type=MESH,
        )

    def weigh(p, it):
        t, pair = it // PAIRS, it % PAIRS
        columns = pl.ds(pl.multiple_of(pair * PAIR, PAIR), PAIR)

        @pl.when(pair == 0)
        def _():
            gather_values(p, t)

        summed = jnp.dot(v_turned[...], probs[t, :, columns], preferred_element_type=jnp.float32)
        if p < 3:
            parts[p][t, 0:BLOCK, columns] = summed

            @pl.when(pair == PAIRS - 1)
            def _():
                part_copy(p, t).start()
        else:
            result = summed * part_far[0, t, BLOCK : BLOCK + 1, columns] + part_far[0, t, 0:BLOCK, columns]
            rows = pl.ds(pl.multiple_of(t * BLOCK, BLOCK), BLOCK)
            out_ref[rows, columns] = jnp.concatenate([result[:, :HD].T, result[:, HD:].T], axis=1).astype(jnp.bfloat16)

    def settle(it, carry):
        t, pair = it // PAIRS, it % PAIRS
        columns = pl.ds(pl.multiple_of(pair * PAIR, PAIR), PAIR)
        stats = [own[t, BLOCK:STATS, columns]] + [part_far[p, t, BLOCK:STATS, columns] for p in range(3)]
        tops, sums = [v[0:1] for v in stats], [v[4:5] for v in stats]
        largest = functools.reduce(jnp.maximum, tops)
        fades = [jnp.exp2((top - largest) * SCALE2) for top in tops]
        denominator = sum(f * v for f, v in zip(fades, sums, strict=True))
        fades = [f / denominator for f in fades]
        rest = part_far[0, t, 0:BLOCK, columns] * fades[1]
        for p in (1, 2):
            rest = rest + part_far[p, t, 0:BLOCK, columns] * fades[p + 1]
        part_far[0, t, 0:BLOCK, columns] = rest
        part_far[0, t, BLOCK:STATS, columns] = jnp.broadcast_to(fades[0], (8, PAIR))
        return carry

    keep(0)
    push_range(0, 1, WINDOW - EARLY + 1)
    loads[1].wait()

    def turn(i):
        pages_v[i] = pages_v[i].astype(jnp.float32).T.astype(jnp.bfloat16)

    def push_and_turn(i, carry):
        push(0, i)
        for n in range(TURNS):
            turn((i - FIRST) * TURNS + n)
        return carry

    lax.fori_loop(FIRST, CTX, push_and_turn, 0)
    for n in range((CTX - FIRST) * TURNS, BLK_DEV):
        turn(n)
    keep(1)
    push_range(1, 1, AHEAD + 1)
    for p in range(4):
        for half in range(2):
            sp = 2 * p + half
            if sp + 2 < 8:
                keep(sp + 2)
            if sp == 7:
                for far in range(3):
                    for t in range(TILE_DEV):
                        part_copy(far, t).wait_recv()
                lax.fori_loop(0, ITEMS, settle, 0)
            arrived(sp)
            if half == 0 and p < 3:
                q_copies[p].wait_recv()

            def work(it, carry, sp=sp, p=p, half=half):
                push_some(sp, it)
                (score if half == 0 else weigh)(p, it)
                return carry

            lax.fori_loop(0, ITEMS, work, 0)

    for p in range(3):
        q_copies[p].wait_send()
        for t in range(TILE_DEV):
            part_copy(p, t).wait_send()

    def drain(w, carry):
        copy_of(0, 1, w).wait_send()
        return carry

    lax.fori_loop(0, WINDOW, drain, 0)


def on_device(queries, keys_cache, values_cache, block_list, page_table):
    wanted, picked = request_plan(page_table[block_list])
    lanes = BLOCK
    ask = jnp.concatenate(
        [
            jnp.pad(wanted, ((0, 0), (0, lanes - CAP))).reshape(PLANES, CTX, lanes),
            jnp.pad(picked, ((0, 0), (0, lanes - TILE_DEV * PER_GRP)))[:, None],
        ],
        axis=1,
    )[:, :, None]
    vmem = pl.BlockSpec(memory_space=pltpu.VMEM)
    whole = pl.BlockSpec(memory_space=pl.ANY)
    half_part = pltpu.VMEM((TILE_DEV, STATS, ROWS), jnp.float32)
    return pl.pallas_call(
        kernel,
        out_shape=jax.ShapeDtypeStruct((TILE_DEV * BLOCK, ROWS), jnp.bfloat16),
        in_specs=[vmem, whole, whole, whole],
        out_specs=vmem,
        scratch_shapes=[
            pltpu.VMEM((TILE_DEV * BLOCK, ROWS), jnp.bfloat16),
            pltpu.VMEM((CTX, 1, BLOCK), jnp.int32),
            pltpu.SMEM((CTX, 1, BLOCK), jnp.int32),
            pltpu.VMEM((BLK_DEV, BLOCK, HD), jnp.bfloat16),
            pltpu.VMEM((BLK_DEV, BLOCK, HD), jnp.bfloat16),
            *[pltpu.VMEM((CTX * CAP, BLOCK, HD), jnp.bfloat16)] * 8,
            pltpu.VMEM((WINDOW, CAP, BLOCK, HD), jnp.bfloat16),
            pltpu.VMEM((3, TILE_DEV * BLOCK, ROWS), jnp.bfloat16),
            pltpu.VMEM((KEYS, PAIR), jnp.float32),
            pltpu.VMEM((TILE_DEV, KEYS, ROWS), jnp.bfloat16),
            pltpu.VMEM((HD, KEYS), jnp.bfloat16),
            half_part,
            half_part,
            half_part,
            half_part,
            pltpu.VMEM((3, TILE_DEV, STATS, ROWS), jnp.float32),
            pltpu.VMEM((PLANES, CTX + 1, 1, BLOCK), jnp.int32),
            pltpu.VMEM((CTX, PLANES, 1, BLOCK), jnp.int32),
            pltpu.SMEM((CTX, PLANES, 1, BLOCK), jnp.int32),
            pltpu.SMEM((PLANES, 1, BLOCK), jnp.int32),
            pltpu.SemaphoreType.DMA((3,)),
            pltpu.SemaphoreType.DMA((WINDOW,)),
            pltpu.SemaphoreType.DMA((8,)),
            pltpu.SemaphoreType.DMA((3,)),
            pltpu.SemaphoreType.DMA((3,)),
            pltpu.SemaphoreType.DMA((3, TILE_DEV)),
            pltpu.SemaphoreType.DMA((3, TILE_DEV)),
            pltpu.SemaphoreType.DMA((4,)),
            pltpu.SemaphoreType.DMA((4,)),
            pltpu.SemaphoreType.DMA((2,)),
            pltpu.SemaphoreType.DMA((3,)),
            pltpu.SemaphoreType.DMA((2,)),
        ],
        compiler_params=pltpu.CompilerParams(
            collective_id=0, has_side_effects=True, vmem_limit_bytes=66_000_000
        ),
    )(ask, queries, keys_cache, values_cache)


def solution(mesh):
    in_specs = (
        P(("grp", "ctx"), None),
        P(("grp", "ctx"), None, None),
        P(("grp", "ctx"), None, None),
        P(("grp", "ctx"), None),
        P(),
    )
    return jax.shard_map(
        on_device, mesh=mesh, in_specs=in_specs, out_specs=P(("grp", "ctx"), None), check_vma=False
    )
```

```python
import functools
import math

import jax
import jax.numpy as jnp
from jax import lax
from jax.experimental import pallas as pl
from jax.experimental.pallas import tpu as pltpu
from jax.sharding import PartitionSpec as P

HD = 128
HEADS = 8
BLOCK = 128
NB = 36
TILE_DEV = 3
BLK_DEV = 128
CAP = 3
PLANES = 4
CTX = 32
PER_GRP = NB // PLANES
KEYS = PER_GRP * BLOCK
ROWS = HEADS * BLOCK
PAIR = 2 * BLOCK
PAIRS = ROWS // PAIR
ITEMS = TILE_DEV * PAIRS
WINDOW = 16
AHEAD = 15
EARLY = 15
OWN_KEYS = 6
FIRST = WINDOW - EARLY + 1
TURNS = BLK_DEV // (32 - FIRST)
PEERS = CTX - 1
PLANE_STEPS = (1, 3, 2, 0)
STATS = BLOCK + 8
MESH = pl.DeviceIdType.MESH
SCALE2 = HD**-0.5 * math.log2(math.e)


def request_plan(page_ids):
    flat = page_ids.reshape(-1)
    device_of, within = flat // BLK_DEV, flat % BLK_DEV
    position = jnp.arange(flat.shape[0], dtype=jnp.int32)
    earlier = position[None, :] < position[:, None]
    rank = jnp.sum(((device_of[None, :] == device_of[:, None]) & earlier).astype(jnp.int32), axis=1)
    devices = jnp.arange(PLANES * CTX, dtype=jnp.int32)
    ranks = jnp.arange(CAP, dtype=jnp.int32)
    place = (device_of * CAP + rank)[None, None, :] == (devices[:, None] * CAP + ranks)[:, :, None]
    wanted = jnp.sum(jnp.where(place, within[None, None, :], 0), axis=2)
    tile = position // NB
    plane = device_of // CTX
    same = (plane[None, :] == plane[:, None]) & (tile[None, :] == tile[:, None]) & earlier
    order = jnp.sum(same.astype(jnp.int32), axis=1)
    slot = (device_of % CTX) * CAP + rank
    key = (plane * TILE_DEV + tile) * PER_GRP + order
    all_keys = jnp.arange(PLANES * TILE_DEV * PER_GRP, dtype=jnp.int32)
    picked = jnp.sum(jnp.where(key[None, :] == all_keys[:, None], slot[None, :], 0), axis=1)
    return wanted, picked.reshape(PLANES, TILE_DEV * PER_GRP)


def kernel(
    ask, q_hbm, k_hbm, v_hbm, out_ref,
    q_ref, near, near_asked,
    pages_k, pages_v, r0, r1, r2, r3, r4, r5, r6, r7,
    stage, q_far, scores, probs, v_turned, own, part0, part1, part2, part_far,
    heard, told, asked, picked,
    load_sem, send_sem, recv_sem, q_send, q_recv, part_send, part_recv, ask_send, ask_recv, tell_sem, near_sem, note_sem,
):
    landed = (r0, r1, r2, r3, r4, r5, r6, r7)
    parts = (part0, part1, part2, own)
    g, c = lax.axis_index("grp"), lax.axis_index("ctx")
    x, y, core = c // 8, (c // 2) % 4, c % 2

    loads = [
        pltpu.make_async_copy(k_hbm, pages_k, load_sem.at[0]),
        pltpu.make_async_copy(v_hbm, pages_v, load_sem.at[1]),
        pltpu.make_async_copy(q_hbm, q_ref, load_sem.at[2]),
    ]
    loads[0].start()
    loads[2].start()
    loads[1].start()

    def walk(n):
        return (1 + 2 * n + n // 2) % 4

    def peer(i):
        far = i // 16
        m = (i + 15 + far) % 16
        a, b = walk(m % 4), walk(m // 4)
        b = b * (1 + 2 * (a // 3)) % 4
        moves = (a + 3) // 4
        b = (b + 2 * core * (moves + (1 - moves) * (b % 2))) % 4
        return (((x + a) % 4) * 4 + (y + b) % 4) * 2 + (core + far) % 2

    barrier = pltpu.get_barrier_semaphore()

    def greet(i, carry):
        pl.semaphore_signal(barrier, inc=1, device_id=(g, peer(i)), device_id_type=MESH)
        return carry

    lax.fori_loop(1, CTX, greet, 0)
    for step in (1, 2, 3):
        pl.semaphore_signal(barrier, inc=1, device_id=((g + step) % 4, c), device_id_type=MESH)
    pl.semaphore_wait(barrier, PEERS + 3)

    def plane_of(p):
        return (g + PLANE_STEPS[p]) % 4

    def number_of(sp, i):
        return sp * PEERS + i - 1 + (EARLY if sp < OWN_KEYS else 0)

    def copy_of(sp, i, number):
        w = number % WINDOW
        return pltpu.make_async_remote_copy(
            src_ref=stage.at[w],
            dst_ref=landed[sp].at[pl.ds(c * CAP, CAP)],
            send_sem=send_sem.at[w],
            recv_sem=recv_sem.at[sp],
            device_id=(g, peer(i)),
            device_id_type=MESH,
        )

    def push(sp, i):
        pages = (pages_k, pages_v)[sp % 2]
        number = number_of(sp, i)

        @pl.when(number >= WINDOW)
        def _():
            copy_of(sp, i, number).wait_send()

        w, who = number % WINDOW, peer(i)
        for r in range(CAP):
            stage[w, r] = pages[asked[who, plane_of(sp // 2), 0, r]]
        copy_of(sp, i, number).start()

    def push_early(i, carry):
        who = peer(i)
        for r in range(CAP):
            stage[i - 1, r] = pages_k[near_asked[who, 0, r]]
        copy_of(OWN_KEYS, i, i - 1).start()
        return carry

    asks = []
    for step in (1, 2, 3):
        asks.append(
            pltpu.make_async_remote_copy(
                src_ref=ask.at[(g + step) % 4],
                dst_ref=heard.at[g],
                send_sem=ask_send.at[step],
                recv_sem=ask_recv.at[step],
                device_id=((g + step) % 4, c),
                device_id_type=MESH,
            )
        )
        asks[-1].start()
    asks.append(pltpu.make_async_copy(ask.at[g], heard.at[g], ask_send.at[0]))
    asks[-1].start()

    def tell_near(i, carry):
        pltpu.make_async_remote_copy(
            src_ref=ask.at[g, peer(i)],
            dst_ref=near.at[c],
            send_sem=near_sem.at[0],
            recv_sem=near_sem.at[1],
            device_id=(g, peer(i)),
            device_id_type=MESH,
        ).start()
        return carry

    own_near = pltpu.make_async_copy(ask.at[g, c], near.at[c], near_sem.at[2])
    own_near.start()
    lax.fori_loop(1, CTX, tell_near, 0)
    for copy in asks:
        copy.wait()

    def tell(i, carry):
        pltpu.make_async_remote_copy(
            src_ref=heard.at[:, peer(i)],
            dst_ref=told.at[c],
            send_sem=tell_sem.at[0],
            recv_sem=tell_sem.at[1],
            device_id=(g, peer(i)),
            device_id_type=MESH,
        ).start()
        return carry

    lax.fori_loop(1, CTX, tell, 0)
    own_list = pltpu.make_async_copy(heard.at[:, c], told.at[c], note_sem.at[0])
    own_picks = pltpu.make_async_copy(heard.at[:, CTX], picked, note_sem.at[1])
    own_list.start()
    own_picks.start()
    for way in range(2):
        everyone = near.at[pl.ds(0, PEERS)]
        pltpu.make_async_copy(everyone, everyone, near_sem.at[way]).wait()
    own_near.wait()
    near_note = pltpu.make_async_copy(near, near_asked, near_sem.at[2])
    near_note.start()
    near_note.wait()
    loads[0].wait()
    lax.fori_loop(1, EARLY + 1, push_early, 0)

    loads[2].wait()

    q_copies = []
    for p in range(3):
        q_copies.append(
            pltpu.make_async_remote_copy(
                src_ref=q_ref,
                dst_ref=q_far.at[p],
                send_sem=q_send.at[p],
                recv_sem=q_recv.at[p],
                device_id=((g + 4 - PLANE_STEPS[p]) % 4, c),
                device_id_type=MESH,
            )
        )
        q_copies[-1].start()

    own_list.wait()
    own_picks.wait()
    for way in range(2):
        everyone = told.at[pl.ds(0, PEERS)]
        pltpu.make_async_copy(everyone, everyone, tell_sem.at[way]).wait()
    note = pltpu.make_async_copy(told, asked, note_sem.at[0])
    note.start()
    note.wait()

    def keep(sp):
        pages = (pages_k, pages_v)[sp % 2]
        for r in range(CAP):
            landed[sp][c * CAP + r] = pages[asked[c, plane_of(sp // 2), 0, r]]

    def push_range(sp, low, high):
        def one(i, carry):
            push(sp, i)
            return carry

        lax.fori_loop(low, high, one, 0)

    def push_some(sp, it):
        if sp + 1 >= 8:
            return

        def one(j, carry):
            n = it * 3 + j

            @pl.when(n < PEERS - AHEAD)
            def _():
                push(sp + 1, AHEAD + 1 + n)

            if sp + 2 < 8:

                begun = EARLY if sp + 2 == OWN_KEYS else 0

                @pl.when((n >= PEERS - AHEAD + begun) & (n < PEERS))
                def _():
                    push(sp + 2, n - (PEERS - AHEAD) + 1)

            return carry

        lax.fori_loop(0, 3, one, 0)

    def arrived(sp):
        everything = landed[sp].at[pl.ds(0, PEERS * CAP)]
        pltpu.make_async_copy(everything, everything, recv_sem.at[sp]).wait()

    def score(p, it):
        t, pair = it // PAIRS, it % PAIRS
        rows = pl.ds(pl.multiple_of(t * BLOCK, BLOCK), BLOCK)
        columns = pl.ds(pl.multiple_of(pair * PAIR, PAIR), PAIR)
        both = q_far[p, rows, columns] if p < 3 else q_ref[rows, columns]
        queries = jnp.concatenate([both[:, :HD], both[:, HD:]], axis=0)
        top = jnp.full((8, PAIR), -jnp.inf, jnp.float32)
        for j in range(PER_GRP):
            keys = landed[2 * p][picked[plane_of(p), 0, t * PER_GRP + j]]
            s = lax.dot_general(keys, queries, (((1,), (1,)), ((), ())), preferred_element_type=jnp.float32)
            scores[j * BLOCK : (j + 1) * BLOCK, :] = s
            top = jnp.maximum(top, jnp.max(s.reshape(BLOCK // 8, 8, PAIR), axis=0))
        largest = jnp.max(top, axis=0, keepdims=True)
        total = jnp.zeros((8, PAIR), jnp.float32)
        for j in range(PER_GRP):
            w = jnp.exp2((scores[j * BLOCK : (j + 1) * BLOCK, :] - largest) * SCALE2)
            total = total + jnp.sum(w.reshape(BLOCK // 8, 8, PAIR), axis=0)
            probs[t, j * BLOCK : (j + 1) * BLOCK, columns] = w.astype(jnp.bfloat16)
        denominator = jnp.sum(total, axis=0, keepdims=True)
        upper = lax.broadcasted_iota(jnp.int32, (8, PAIR), 0) < 4
        parts[p][t, BLOCK:STATS, columns] = jnp.where(upper, largest, denominator)

    def gather_values(p, t):
        for j in range(PER_GRP):
            v_turned[:, j * BLOCK : (j + 1) * BLOCK] = landed[2 * p + 1][picked[plane_of(p), 0, t * PER_GRP + j]]

    def part_copy(p, t):
        return pltpu.make_async_remote_copy(
            src_ref=parts[p].at[t],
            dst_ref=part_far.at[p, t],
            send_sem=part_send.at[p, t],
            recv_sem=part_recv.at[p, t],
            device_id=(plane_of(p), c),
            device_id_type=MESH,
        )

    def weigh(p, it):
        t, pair = it // PAIRS, it % PAIRS
        columns = pl.ds(pl.multiple_of(pair * PAIR, PAIR), PAIR)

        @pl.when(pair == 0)
        def _():
            gather_values(p, t)

        summed = jnp.dot(v_turned[...], probs[t, :, columns], preferred_element_type=jnp.float32)
        if p < 3:
            parts[p][t, 0:BLOCK, columns] = summed

            @pl.when(pair == PAIRS - 1)
            def _():
                part_copy(p, t).start()
        else:
            result = summed * part_far[0, t, BLOCK : BLOCK + 1, columns] + part_far[0, t, 0:BLOCK, columns]
            rows = pl.ds(pl.multiple_of(t * BLOCK, BLOCK), BLOCK)
            out_ref[rows, columns] = jnp.concatenate([result[:, :HD].T, result[:, HD:].T], axis=1).astype(jnp.bfloat16)

    def settle(it, carry):
        t, pair = it // PAIRS, it % PAIRS
        columns = pl.ds(pl.multiple_of(pair * PAIR, PAIR), PAIR)
        stats = [own[t, BLOCK:STATS, columns]] + [part_far[p, t, BLOCK:STATS, columns] for p in range(3)]
        tops, sums = [v[0:1] for v in stats], [v[4:5] for v in stats]
        largest = functools.reduce(jnp.maximum, tops)
        fades = [jnp.exp2((top - largest) * SCALE2) for top in tops]
        denominator = sum(f * v for f, v in zip(fades, sums, strict=True))
        fades = [f / denominator for f in fades]
        rest = part_far[0, t, 0:BLOCK, columns] * fades[1]
        for p in (1, 2):
            rest = rest + part_far[p, t, 0:BLOCK, columns] * fades[p + 1]
        part_far[0, t, 0:BLOCK, columns] = rest
        part_far[0, t, BLOCK:STATS, columns] = jnp.broadcast_to(fades[0], (8, PAIR))
        return carry

    keep(0)
    push_range(0, 1, WINDOW - EARLY + 1)
    loads[1].wait()

    def turn(i):
        pages_v[i] = pages_v[i].astype(jnp.float32).T.astype(jnp.bfloat16)

    def push_and_turn(i, carry):
        push(0, i)
        for n in range(TURNS):
            turn((i - FIRST) * TURNS + n)
        return carry

    lax.fori_loop(FIRST, CTX, push_and_turn, 0)
    for n in range((CTX - FIRST) * TURNS, BLK_DEV):
        turn(n)
    keep(1)
    push_range(1, 1, AHEAD + 1)
    for p in range(4):
        for half in range(2):
            sp = 2 * p + half
            if sp + 2 < 8:
                keep(sp + 2)
            if sp == 7:
                for far in range(3):
                    for t in range(TILE_DEV):
                        part_copy(far, t).wait_recv()
                lax.fori_loop(0, ITEMS, settle, 0)
            arrived(sp)
            if half == 0 and p < 3:
                q_copies[p].wait_recv()

            def work(it, carry, sp=sp, p=p, half=half):
                push_some(sp, it)
                (score if half == 0 else weigh)(p, it)
                return carry

            lax.fori_loop(0, ITEMS, work, 0)

    for p in range(3):
        q_copies[p].wait_send()
        for t in range(TILE_DEV):
            part_copy(p, t).wait_send()

    def drain(w, carry):
        copy_of(0, 1, w).wait_send()
        return carry

    lax.fori_loop(0, WINDOW, drain, 0)


def on_device(queries, keys_cache, values_cache, block_list, page_table):
    wanted, picked = request_plan(page_table[block_list])
    lanes = BLOCK
    ask = jnp.concatenate(
        [
            jnp.pad(wanted, ((0, 0), (0, lanes - CAP))).reshape(PLANES, CTX, lanes),
            jnp.pad(picked, ((0, 0), (0, lanes - TILE_DEV * PER_GRP)))[:, None],
        ],
        axis=1,
    )[:, :, None]
    vmem = pl.BlockSpec(memory_space=pltpu.VMEM)
    whole = pl.BlockSpec(memory_space=pl.ANY)
    half_part = pltpu.VMEM((TILE_DEV, STATS, ROWS), jnp.float32)
    return pl.pallas_call(
        kernel,
        out_shape=jax.ShapeDtypeStruct((TILE_DEV * BLOCK, ROWS), jnp.bfloat16),
        in_specs=[vmem, whole, whole, whole],
        out_specs=vmem,
        scratch_shapes=[
            pltpu.VMEM((TILE_DEV * BLOCK, ROWS), jnp.bfloat16),
            pltpu.VMEM((CTX, 1, BLOCK), jnp.int32),
            pltpu.SMEM((CTX, 1, BLOCK), jnp.int32),
            pltpu.VMEM((BLK_DEV, BLOCK, HD), jnp.bfloat16),
            pltpu.VMEM((BLK_DEV, BLOCK, HD), jnp.bfloat16),
            *[pltpu.VMEM((CTX * CAP, BLOCK, HD), jnp.bfloat16)] * 8,
            pltpu.VMEM((WINDOW, CAP, BLOCK, HD), jnp.bfloat16),
            pltpu.VMEM((3, TILE_DEV * BLOCK, ROWS), jnp.bfloat16),
            pltpu.VMEM((KEYS, PAIR), jnp.float32),
            pltpu.VMEM((TILE_DEV, KEYS, ROWS), jnp.bfloat16),
            pltpu.VMEM((HD, KEYS), jnp.bfloat16),
            half_part,
            half_part,
            half_part,
            half_part,
            pltpu.VMEM((3, TILE_DEV, STATS, ROWS), jnp.float32),
            pltpu.VMEM((PLANES, CTX + 1, 1, BLOCK), jnp.int32),
            pltpu.VMEM((CTX, PLANES, 1, BLOCK), jnp.int32),
            pltpu.SMEM((CTX, PLANES, 1, BLOCK), jnp.int32),
            pltpu.SMEM((PLANES, 1, BLOCK), jnp.int32),
            pltpu.SemaphoreType.DMA((3,)),
            pltpu.SemaphoreType.DMA((WINDOW,)),
            pltpu.SemaphoreType.DMA((8,)),
            pltpu.SemaphoreType.DMA((3,)),
            pltpu.SemaphoreType.DMA((3,)),
            pltpu.SemaphoreType.DMA((3, TILE_DEV)),
            pltpu.SemaphoreType.DMA((3, TILE_DEV)),
            pltpu.SemaphoreType.DMA((4,)),
            pltpu.SemaphoreType.DMA((4,)),
            pltpu.SemaphoreType.DMA((2,)),
            pltpu.SemaphoreType.DMA((3,)),
            pltpu.SemaphoreType.DMA((2,)),
        ],
        compiler_params=pltpu.CompilerParams(
            collective_id=0, has_side_effects=True, vmem_limit_bytes=66_000_000
        ),
    )(ask, queries, keys_cache, values_cache)


def solution(mesh):
    in_specs = (
        P(("grp", "ctx"), None),
        P(("grp", "ctx"), None, None),
        P(("grp", "ctx"), None, None),
        P(("grp", "ctx"), None),
        P(),
    )
    return jax.shard_map(
        on_device, mesh=mesh, in_specs=in_specs, out_specs=P(("grp", "ctx"), None), check_vma=False
    )
```
